32 devices in a mesh: dev: 32 (over z, y, x, core).
Axes of the slice: x: 2, y: 2, z: 4, core: 2. Of those that a mesh axis runs over, the one named last changes fastest.
Arguments:
- tokens: bfloat16 [16384, 768], P('dev'), may hold values from -6 to 6
- segments: int32 [16384], P('dev'), may hold values from 0 to 31, as said below
- w_qkv: bfloat16 [768, 2304], P('dev'), may hold values from -0.21875 to 0.21875
- bias_query: bfloat16 [768], P('dev'), may hold values from -3 to 3
- bias_value: bfloat16 [768], P('dev'), may hold values from -3 to 3
- w_out: bfloat16 [768, 768], P('dev'), may hold values from -2.5 to 2.5
- bias_out: bfloat16 [768], P('dev'), may hold values from -3 to 3
- w_up: bfloat16 [768, 3072], P('dev'), may hold values from -0.21875 to 0.21875
- bias_up: bfloat16 [3072], P('dev'), may hold values from -3 to 3
- w_down: bfloat16 [3072, 768], P('dev'), may hold values from -0.109375 to 0.109375
- bias_down: bfloat16 [768], P('dev'), may hold values from -3 to 3
- norm1_gain: bfloat16 [768], P('dev'), may hold values from 0.5 to 2
- norm1_shift: bfloat16 [768], P('dev'), may hold values from -3 to 3
- norm2_gain: bfloat16 [768], P('dev'), may hold values from 0.5 to 2
- norm2_shift: bfloat16 [768], P('dev'), may hold values from -3 to 3
- grad_out: bfloat16 [16384, 768], P('dev'), may hold values from -6 to 6
Outputs:
- result: bfloat16 [16384, 768], P('dev')
- d_tokens: bfloat16 [16384, 768], P('dev')
- grad_w_qkv: float32 [768, 2304], P('dev')
- grad_bias_query: float32 [768], P('dev')
- grad_bias_value: float32 [768], P('dev')
- grad_w_out: float32 [768, 768], P('dev')
- grad_bias_out: float32 [768], P('dev')
- grad_w_up: float32 [768, 3072], P('dev')
- grad_bias_up: float32 [3072], P('dev')
- grad_w_down: float32 [3072, 768], P('dev')
- grad_bias_down: float32 [768], P('dev')
- grad_norm1_gain: float32 [768], P('dev')
- grad_norm1_shift: float32 [768], P('dev')
- grad_norm2_gain: float32 [768], P('dev')
- grad_norm2_shift: float32 [768], P('dev')
The draws below stay inside these ranges and needn't reach their ends.
Inputs may be any that keep to these rules, and one draw needn't show every extreme that they name: `segments`: tokens of the r-th aligned block of 1024 tokens carry 2 r for the frames of its clip, which starts at the block's first token, and 2 r + 1 for the padding after it; a clip has 768 to 1023 frames, both bounds reached in every draw.
All inputs are finite; a program needn't handle non-finite values.
Results may differ from the reference program's by a relative error of at most 0.013.
The reference program's roundings to bfloat16 on the way count: a program that leaves them out, or rounds other values in their place, can miss the bound.
Values may be sent and summed in bfloat16 or wider, within the bound.
No kernel may reach another device: no remote copies, remote signals or barrier semaphores. Data moves between devices by JAX's collectives and lax.ppermute only.
A program may use at most 192 MiB of HBM per device.

```python
import math
from functools import partial
import jax
import jax.numpy as jnp
from jax import lax

D = 768
HEADS = 12
HEAD_DIM = 64
FF = 3072
REGION = 1024
REGIONS = 16
TOKENS = 16384


def draw_segments(key, part):
    shortest = 3 * REGION // 4
    clip_lengths = jax.random.randint(key, (REGIONS,), shortest, REGION).astype(jnp.int32)
    clip_lengths = clip_lengths.at[0].set(shortest).at[REGIONS - 1].set(REGION - 1)
    position = jnp.arange(TOKENS, dtype=jnp.int32)
    region_of = position // REGION
    within = position % REGION
    limits = clip_lengths[region_of]
    return (2 * region_of + (within >= limits).astype(jnp.int32)).astype(jnp.int32)


def shard_levels(rng, extent, cuts, least, top_value):
    def one(axis_at, parts):
        draws = jax.random.uniform(jax.random.fold_in(jax.random.fold_in(rng, 6), axis_at), (parts,), jnp.float32, least / len(cuts), top_value / len(cuts))
        return jnp.repeat(jnp.exp(draws), extent[axis_at] // parts).reshape((-1,) + (1,) * (len(extent) - axis_at - 1))

    loudness = one(*cuts[0])
    for cut in cuts[1:]:
        loudness = loudness * one(*cut)
    return loudness


def scatter_about(key, shape, scale, most, cuts=(), kind=jnp.bfloat16):
    factor_of = shard_levels(key, shape, cuts, -0.22, 0.18) if cuts else 1.0
    drawn = jax.random.normal(key, shape, jnp.float32) * scale * factor_of
    return jnp.minimum(jnp.maximum(drawn, -most), most).astype(kind)


def setup_inputs(seed: int = 0) -> dict:
    arg_keys = jax.random.split(jax.random.key(seed), 17)
    tokens = scatter_about(arg_keys[0], (TOKENS, D), 1.0, 6.0, ((0, 32),))
    segments = draw_segments(jax.random.fold_in(arg_keys[16], 71), 0)
    w_qkv = scatter_about(arg_keys[2], (D, 3 * D), D ** -0.5, 0.21875, ((0, 32),))
    bias_query = scatter_about(arg_keys[3], (D,), 0.5, 3.0, ((0, 32),))
    bias_value = scatter_about(arg_keys[4], (D,), 0.5, 3.0, ((0, 32),))
    w_out = scatter_about(arg_keys[5], (D, D), (D // 128) ** -0.5, 2.5, ((0, 32),))
    bias_out = scatter_about(arg_keys[6], (D,), 0.5, 3.0, ((0, 32),))
    w_up = scatter_about(arg_keys[7], (D, FF), D ** -0.5, 0.21875, ((0, 32),))
    bias_up = scatter_about(arg_keys[8], (FF,), 0.5, 3.0, ((0, 32),))
    w_down = scatter_about(arg_keys[9], (FF, D), FF ** -0.5, 0.109375, ((0, 32),))
    bias_down = scatter_about(arg_keys[10], (D,), 0.5, 3.0, ((0, 32),))
    norm1_gain = jnp.clip(jnp.exp(math.log(2.0) - 1.3862944 * jax.random.uniform(arg_keys[11], (D,), jnp.float32) ** shard_levels(arg_keys[11], (D,), ((0, 32),), -0.2, 0.2)), 0.5, 2.0).astype(jnp.bfloat16)
    norm1_shift = scatter_about(arg_keys[12], (D,), 0.5, 3.0, ((0, 32),))
    norm2_gain = jnp.clip(jnp.exp(math.log(2.0) - 1.3862944 * jax.random.uniform(arg_keys[13], (D,), jnp.float32) ** shard_levels(arg_keys[13], (D,), ((0, 32),), -0.2, 0.2)), 0.5, 2.0).astype(jnp.bfloat16)
    norm2_shift = scatter_about(arg_keys[14], (D,), 0.5, 3.0, ((0, 32),))
    grad_out = scatter_about(arg_keys[15], (TOKENS, D), 1.0, 6.0, ((0, 32),))
    return dict(tokens=tokens, segments=segments, w_qkv=w_qkv, bias_query=bias_query, bias_value=bias_value, w_out=w_out, bias_out=bias_out, w_up=w_up, bias_up=bias_up, w_down=w_down, bias_down=bias_down, norm1_gain=norm1_gain, norm1_shift=norm1_shift, norm2_gain=norm2_gain, norm2_shift=norm2_shift, grad_out=grad_out)


@jax.custom_vjp
def low(v):
    return lax.optimization_barrier(v.astype(jnp.bfloat16)).astype(jnp.float32)

@jax.custom_vjp
def low_back(v):
    return v

def low_keep(v):
    return (low(v), None)

def low_pass(kept, grad):
    return (grad,)

def back_keep(v):
    return (v, None)

def back_low(kept, grad):
    return (low(grad),)
low.defvjp(low_keep, low_pass)
low_back.defvjp(back_keep, back_low)
epsilon = 1e-05

def layer_norm(inputs, norm_gain, norm_shift):
    average = lax.optimization_barrier(jnp.mean(inputs, axis=-1, keepdims=True))
    centred = inputs - average
    variance = lax.optimization_barrier(jnp.mean(centred * centred, axis=-1, keepdims=True))
    return centred * lax.rsqrt(variance + epsilon) * norm_gain + norm_shift

def gelu_exact(inputs):
    return 0.5 * inputs * (1.0 + lax.erf(inputs * 0.7071067811865476))

def matmul(left, right):
    return jnp.dot(left, right, precision=lax.Precision.HIGHEST)

def clip_attention(queries, keys, values, seg_ids):
    scores = jnp.einsum('qhd,khd->hqk', queries, keys, precision=lax.Precision.HIGHEST)
    scores = low_back(scores * HEAD_DIM ** (-0.5))
    allowed = seg_ids[:, None] == seg_ids[None, :]
    scores = jnp.where(allowed[None], scores, -1000000000.0)
    highest = lax.optimization_barrier(jnp.max(scores, axis=-1, keepdims=True))
    raised = jnp.exp(scores - highest)
    probs = low(raised / lax.optimization_barrier(jnp.sum(raised, axis=-1, keepdims=True)))
    return jnp.einsum('hqk,khd->qhd', probs, values, precision=lax.Precision.HIGHEST)

def attend(queries, keys, values, segments):
    shape_four = (REGIONS, REGION, HEADS, HEAD_DIM)
    blocked = jax.checkpoint(clip_attention)

    def region_step(carry, items):
        return (carry, blocked(items[0], items[1], items[2], items[3]))
    _, mixed = lax.scan(region_step, jnp.zeros((), jnp.float32), (queries.reshape(shape_four), keys.reshape(shape_four), values.reshape(shape_four), segments.reshape(REGIONS, REGION)))
    return mixed.reshape(TOKENS, HEADS * HEAD_DIM)

def forward(segments, inputs, w_qkv, bias_query, bias_value, w_out, bias_out, w_up, bias_up, w_down, bias_down, norm1_gain, norm1_shift, norm2_gain, norm2_shift):
    act_one = low(layer_norm(inputs, norm1_gain, norm1_shift))
    projected = matmul(act_one, w_qkv)
    queries = low_back(low(projected[:, :D] + bias_query))
    keys = low_back(low(projected[:, D:2 * D]))
    values = low_back(low(projected[:, 2 * D:] + bias_value))
    mixed = low_back(low(attend(queries, keys, values, segments)))
    branch = low_back(matmul(mixed, w_out) + bias_out)
    middle = inputs + branch
    act_two = low(layer_norm(middle, norm2_gain, norm2_shift))
    pre_gate = low_back(matmul(act_two, w_up) + bias_up)
    hidden = low(gelu_exact(pre_gate))
    return middle + matmul(hidden, w_down) + bias_down

def reference(tokens, segments, w_qkv, bias_query, bias_value, w_out, bias_out, w_up, bias_up, w_down, bias_down, norm1_gain, norm1_shift, norm2_gain, norm2_shift, grad_out):
    floats = [item.astype(jnp.float32) for item in (tokens, w_qkv, bias_query, bias_value, w_out, bias_out, w_up, bias_up, w_down, bias_down, norm1_gain, norm1_shift, norm2_gain, norm2_shift)]
    output, pullback = jax.vjp(partial(forward, segments), *floats)
    grads = pullback(grad_out.astype(jnp.float32))
    return (output.astype(jnp.bfloat16), grads[0].astype(jnp.bfloat16), grads[1], grads[2], grads[3], grads[4], grads[5], grads[6], grads[7], grads[8], grads[9], grads[10], grads[11], grads[12], grads[13])
```

```python
import math
import jax
import jax.numpy as jnp
from jax import lax
from jax.experimental import pallas as pl
from jax.experimental.pallas import tpu as pltpu
from jax.sharding import PartitionSpec as P

HEAD_DIM = 64
LANES = 128
FAR = float(2**40)
epsilon = 1e-05
f32, bf16 = jnp.float32, jnp.bfloat16


def dot(a, b):
    return jnp.dot(a, b, preferred_element_type=f32)


def dot_nt(a, b):
    return lax.dot_general(a, b, (((1,), (1,)), ((), ())), preferred_element_type=f32)


def dot_tn(a, b):
    return lax.dot_general(a, b, (((0,), (0,)), ((), ())), preferred_element_type=f32)


def column_sum(matrix):
    return jnp.sum(matrix.astype(f32), axis=0)


def partner(value):
    return lax.ppermute(value, "dev", [(i, i ^ 1) for i in range(lax.axis_size("dev"))])


def in_order(core, mine, other, axis):
    return jnp.where(
        core == 0,
        jnp.concatenate([mine, other], axis=axis),
        jnp.concatenate([other, mine], axis=axis),
    )


def stage_masks(n):
    bits = int(math.log2(n)) - 1
    stages = [(1 << b, 1 << b) for b in range(bits, 2, -1)]
    if bits >= 2:
        stages += [(2, 4), (4, 2)]
    elif bits == 1:
        stages += [(2, 2)]
    return stages


def flip(value, masks):
    n = lax.axis_size("dev")
    return lax.ppermute(value, "dev", [(i, i ^ masks[i & 1]) for i in range(n)])


def positions(dev, core, n):
    stages = stage_masks(n)
    tables = []
    for k in range(2):
        row = []
        for j in range(n // 2):
            m = 0
            for s, masks in enumerate(stages):
                if j >> s & 1:
                    m |= masks[k]
            row.append(m)
        tables.append(row)
    both = jnp.asarray(tables, jnp.int32)
    return jnp.right_shift(jnp.bitwise_xor(dev, jnp.where(core == 0, both[0], both[1])), 1)


def column_block(width):
    best = LANES
    for c in range(LANES, 641, LANES):
        if width % c == 0:
            best = c
    return best


def place_kernel(pos_ref, *refs):
    out = refs[-1]
    j = 0
    for ref in refs[:-1]:
        for b in range(ref.shape[0]):
            out[pos_ref[j]] = ref[b]
            j += 1


def place(pieces, pos):
    rows, width = pieces[0].shape[1:]
    chips = sum(p.shape[0] for p in pieces)
    cb = column_block(width)
    return pl.pallas_call(
        place_kernel,
        out_shape=jax.ShapeDtypeStruct((chips, rows, width), pieces[0].dtype),
        grid_spec=pltpu.PrefetchScalarGridSpec(
            num_scalar_prefetch=1,
            grid=(width // cb,),
            in_specs=[
                pl.BlockSpec((p.shape[0], rows, cb), lambda i, t: (0, 0, i)) for p in pieces
            ],
            out_specs=pl.BlockSpec((chips, rows, cb), lambda i, t: (0, 0, i)),
        ),
        cost_estimate=pl.CostEstimate(
            flops=0, transcendentals=0, bytes_accessed=4 * chips * rows * width
        ),
        name="place",
    )(pos, *pieces)


def pick_kernel(pos_ref, ref, keep, send):
    half = keep.shape[0]
    for j in range(half):
        keep[j] = ref[pos_ref[j]]
        send[j] = ref[pos_ref[half + j]]


def pick(blocks, pos):
    chips, rows, width = blocks.shape
    cb = column_block(width)
    half = jax.ShapeDtypeStruct((chips // 2, rows, width), blocks.dtype)
    half_spec = pl.BlockSpec((chips // 2, rows, cb), lambda i, t: (0, 0, i))
    return pl.pallas_call(
        pick_kernel,
        out_shape=(half, half),
        grid_spec=pltpu.PrefetchScalarGridSpec(
            num_scalar_prefetch=1,
            grid=(width // cb,),
            in_specs=[pl.BlockSpec((chips, rows, cb), lambda i, t: (0, 0, i))],
            out_specs=(half_spec, half_spec),
        ),
        cost_estimate=pl.CostEstimate(
            flops=0, transcendentals=0, bytes_accessed=4 * chips * rows * width
        ),
        name="pick",
    )(pos, blocks)


def gather_chips(block, pos):
    n = lax.axis_size("dev")
    pieces = [block[None]]
    for masks in stage_masks(n):
        held = pieces[0] if len(pieces) == 1 else jnp.concatenate(pieces, axis=0)
        pieces.append(flip(held, masks))
    whole = place(pieces, pos)
    return whole.reshape(-1, block.shape[1])


def scatter_chips(matrix, pos):
    n = lax.axis_size("dev")
    chips = n // 2
    keep, send = pick(matrix.reshape(chips, -1, matrix.shape[1]), pos)
    stages = stage_masks(n)
    for s in reversed(range(len(stages))):
        came = flip(send, stages[s])
        total = keep.astype(f32) + came.astype(f32)
        half = total.shape[0] // 2
        if s == 0:
            return total[0]
        send = total[half:].astype(bf16)
        keep = total[:half]


ROWS = 256


def attend_kernel(q_ref, k_ref, v_ref, qs_ref, ks_ref, o_ref, p_ref):
    q, k, v = q_ref[...], k_ref[...], v_ref[...]
    qs, ks = qs_ref[...], ks_ref[...]
    q_low = lax.broadcasted_iota(jnp.int32, q.shape, 1) < HEAD_DIM
    k_low = lax.broadcasted_iota(jnp.int32, k.shape, 1) < HEAD_DIM
    outs = []
    for h in range(2):
        qh = jnp.where(q_low, q, qs) if h == 0 else jnp.where(q_low, qs, q)
        kh = jnp.where(k_low, k, ks) if h == 0 else jnp.where(k_low, ks, k)
        s = dot_nt(qh, kh)
        e = jnp.exp(s - jnp.max(s, axis=-1, keepdims=True))
        p = (e * (1.0 / jnp.sum(e, axis=-1, keepdims=True))).astype(bf16)
        p_ref[h] = p
        outs.append(dot(p, v))
    o_ref[...] = jnp.where(q_low, outs[0], outs[1]).astype(bf16)


def attend_pair(qkv, seg_q, seg_k, pair, pairs):
    rows = qkv.shape[0]
    r = min(ROWS, rows)
    return pl.pallas_call(
        attend_kernel,
        out_shape=(
            jax.ShapeDtypeStruct((rows, LANES), bf16),
            jax.ShapeDtypeStruct((2, rows, rows), bf16),
        ),
        grid=(rows // r,),
        in_specs=[
            pl.BlockSpec((r, LANES), lambda i: (i, pair)),
            pl.BlockSpec((rows, LANES), lambda i: (0, pairs + pair)),
            pl.BlockSpec((rows, LANES), lambda i: (0, 2 * pairs + pair)),
            pl.BlockSpec((r, LANES), lambda i: (i, 0)),
            pl.BlockSpec((rows, LANES), lambda i: (0, 0)),
        ],
        out_specs=(
            pl.BlockSpec((r, LANES), lambda i: (i, 0)),
            pl.BlockSpec((2, r, rows), lambda i: (0, i, 0)),
        ),
        cost_estimate=pl.CostEstimate(
            flops=2 * 2 * 2 * rows * rows * 256,
            transcendentals=2 * rows * rows,
            bytes_accessed=4 * rows * rows,
        ),
        name="attend",
    )(qkv, qkv, qkv, seg_q, seg_k)


def attend_back_kernel(q_ref, k_ref, v_ref, p_ref, do_ref, dq_ref, dk_ref, dv_ref, kt, vt):
    step = pl.program_id(0)

    @pl.when(step == 0)
    def _():
        kt[...] = jnp.zeros_like(kt)
        vt[...] = jnp.zeros_like(vt)

    q, k, v, do = q_ref[...], k_ref[...], v_ref[...], do_ref[...]
    low = lax.broadcasted_iota(jnp.int32, q.shape, 1) < HEAD_DIM
    zero = jnp.zeros_like(q)
    dqs = []
    for h in range(2):
        qh = jnp.where(low, q, zero) if h == 0 else jnp.where(low, zero, q)
        doh = jnp.where(low, do, zero) if h == 0 else jnp.where(low, zero, do)
        p = p_ref[h]
        dp = dot_nt(doh, v)
        pf = p.astype(f32)
        delta = jnp.sum(pf * dp, axis=-1, keepdims=True)
        ds = (pf * (dp - delta)).astype(bf16)
        dqs.append(dot(ds, k))
        vt[...] += dot_tn(doh, p)
        kt[...] += dot_tn(qh, ds)
    dq_ref[...] = (jnp.where(low, dqs[0], dqs[1]) * HEAD_DIM ** (-0.5)).astype(bf16)

    @pl.when(step == pl.num_programs(0) - 1)
    def _():
        dk_ref[...] = kt[...].T.astype(bf16)
        dv_ref[...] = vt[...].T.astype(bf16)


def attend_back_pair(qkv, probs, d_mixed, pair, pairs):
    rows = qkv.shape[0]
    r = min(ROWS, rows)
    col = jax.ShapeDtypeStruct((rows, LANES), bf16)
    return pl.pallas_call(
        attend_back_kernel,
        out_shape=(col, col, col),
        grid=(rows // r,),
        in_specs=[
            pl.BlockSpec((r, LANES), lambda i: (i, pair)),
            pl.BlockSpec((rows, LANES), lambda i: (0, pairs + pair)),
            pl.BlockSpec((rows, LANES), lambda i: (0, 2 * pairs + pair)),
            pl.BlockSpec((2, r, rows), lambda i: (0, i, 0)),
            pl.BlockSpec((r, LANES), lambda i: (i, pair)),
        ],
        out_specs=(
            pl.BlockSpec((r, LANES), lambda i: (i, 0)),
            pl.BlockSpec((rows, LANES), lambda i: (0, 0)),
            pl.BlockSpec((rows, LANES), lambda i: (0, 0)),
        ),
        scratch_shapes=[pltpu.VMEM((LANES, rows), f32), pltpu.VMEM((LANES, rows), f32)],
        cost_estimate=pl.CostEstimate(
            flops=2 * 4 * 2 * rows * rows * 256,
            transcendentals=0,
            bytes_accessed=4 * rows * rows,
        ),
        name="attend_back",
    )(qkv, qkv, qkv, probs, d_mixed)


def normalize(x):
    centred = x - jnp.mean(x, axis=-1, keepdims=True)
    r = lax.rsqrt(jnp.mean(centred * centred, axis=-1, keepdims=True) + epsilon)
    return centred * r, r


def norm_back(d_act, normed, r, gain):
    e = d_act * gain
    m = jnp.mean(e, axis=-1, keepdims=True)
    c = jnp.mean(e * normed, axis=-1, keepdims=True)
    return r * (e - m - normed * c)


def on_device(
    tokens,
    segments,
    w_qkv,
    bias_query,
    bias_value,
    w_out,
    bias_out,
    w_up,
    bias_up,
    w_down,
    bias_down,
    norm1_gain,
    norm1_shift,
    norm2_gain,
    norm2_shift,
    grad_out,
):
    n = lax.axis_size("dev")
    chips = n // 2
    dev = lax.axis_index("dev")
    core = jnp.bitwise_and(dev, 1)
    pos = positions(dev, core, n)
    own, width = tokens.shape
    rows = w_qkv.shape[0]
    strip = w_down.shape[0]
    half = width // 2
    ff_half = w_up.shape[1] // 2
    pairs = half // LANES

    tokens_all = jnp.concatenate([tokens, partner(tokens)], axis=0)
    seg_all = jnp.concatenate([segments, partner(segments)], axis=0)
    grad_all = jnp.concatenate([grad_out, partner(grad_out)], axis=0)

    qkv4 = w_qkv.reshape(rows, 3, 2, half)
    up4 = w_up.reshape(rows, chips, 2, strip)
    out3 = w_out.reshape(rows, 2, half)

    def column_half(k):
        return jnp.concatenate(
            [
                qkv4[:, :, k].reshape(rows, 3 * half),
                out3[:, k],
                up4[:, :, k].reshape(rows, ff_half),
            ],
            axis=1,
        )

    zero_half, one_half = column_half(0), column_half(1)
    vectors = jnp.stack(
        [
            bias_query,
            bias_value,
            bias_out,
            bias_down,
            norm1_gain,
            norm1_shift,
            norm2_gain,
            norm2_shift,
        ],
        axis=1,
    )
    vectors = jnp.pad(vectors, ((0, 0), (0, LANES - 8)))
    mine = jnp.concatenate([jnp.where(core == 0, zero_half, one_half), vectors], axis=1)
    other = jnp.concatenate([jnp.where(core == 0, one_half, zero_half), vectors], axis=1)
    block = in_order(core, mine, partner(other), 0)
    chip_rows = 2 * rows
    per_row = strip // chip_rows
    vec_block = jnp.concatenate(
        [
            block[:, 4 * width : 4 * width + 8],
            bias_up.reshape(chip_rows, per_row),
            jnp.zeros((chip_rows, LANES - 8 - per_row), bf16),
        ],
        axis=1,
    )
    first = jnp.concatenate([block[:, : 3 * half], vec_block], axis=1)
    second = block[:, 3 * half : 4 * width]

    first_all = gather_chips(first, pos)
    qkv_w = first_all[:, : 3 * half]
    vec_all = first_all[:, 3 * half :].astype(f32)
    vec_t = vec_all.T
    bq, bv, bo, bd, gain_one, shift_one, gain_two, shift_two = (vec_t[j] for j in range(8))
    bu = vec_all[:, 8 : 8 + per_row].reshape(ff_half)

    def core_half(v):
        return jnp.where(core == 0, v[..., :half], v[..., half:])

    inputs = tokens_all.astype(f32)
    normed_one, r_one = normalize(inputs)
    act_one = (normed_one * gain_one + shift_one).astype(bf16)
    bias_qkv = jnp.concatenate([core_half(bq), jnp.zeros((half,), f32), core_half(bv)])
    factor = jnp.concatenate(
        [jnp.full((half,), HEAD_DIM ** (-0.5), f32), jnp.ones((2 * half,), f32)]
    )
    qkv = (dot(act_one, qkv_w) + bias_qkv).astype(bf16)
    qkv = (qkv.astype(f32) * factor).astype(bf16)

    second_all = gather_chips(second, pos)
    down_w = gather_chips(w_down, pos)
    out_mine = second_all[:, :half]
    up_w = second_all[:, half:]
    out_w = in_order(core, out_mine, partner(out_mine), 1)

    odd = jnp.bitwise_and(seg_all, 1).astype(f32)[:, None]
    lane = lax.broadcasted_iota(jnp.int32, (1, LANES), 1) % HEAD_DIM
    seg_q = jnp.where(lane == 0, odd, jnp.where(lane == 1, 1.0 - odd, 0.0)).astype(bf16)
    seg_k = jnp.where(
        lane == 0, -FAR * (1.0 - odd), jnp.where(lane == 1, -FAR * odd, 0.0)
    ).astype(bf16)

    heads = [attend_pair(qkv, seg_q, seg_k, p, pairs) for p in range(pairs)]
    mixed_heads = jnp.concatenate([h[0] for h in heads], axis=1)
    mixed = in_order(core, mixed_heads[:own], partner(mixed_heads[own:]), 1)
    middle = tokens.astype(f32) + dot(mixed, out_w) + bo
    normed_two, r_two = normalize(middle)
    act_two = (normed_two * gain_two + shift_two).astype(bf16)
    act_two_all = jnp.concatenate([act_two, partner(act_two)], axis=0)
    pre_gate = dot(act_two_all, up_w) + bu
    cdf = 0.5 * (1.0 + lax.erf(pre_gate * 0.7071067811865476))
    hidden = (pre_gate * cdf).astype(bf16)

    d_hidden = dot_nt(grad_all, down_w)
    slope = cdf + pre_gate * jnp.exp(-0.5 * pre_gate * pre_gate) * 0.3989422804014327
    d_pre = (slope * d_hidden).astype(bf16)
    grad_down = scatter_chips(dot_tn(hidden, grad_all).astype(bf16), pos)

    d_two_part = dot_nt(d_pre, up_w)
    d_act_two = d_two_part[:own] + partner(d_two_part[own:])
    grad_bias_up = column_sum(d_pre)
    grad_up_part = dot_tn(act_two_all, d_pre).astype(bf16)
    grad_gain_two = jnp.sum(d_act_two * normed_two, axis=0)
    grad_shift_two = jnp.sum(d_act_two, axis=0)
    d_middle = grad_out.astype(f32) + norm_back(d_act_two, normed_two, r_two, gain_two)
    d_branch = d_middle.astype(bf16)
    grad_bias_out = column_sum(d_branch)
    d_mixed_rows = dot_nt(d_branch, out_w).astype(bf16)
    d_mixed = jnp.concatenate(
        [
            core_half(d_mixed_rows),
            partner(jnp.where(core == 0, d_mixed_rows[:, half:], d_mixed_rows[:, :half])),
        ],
        axis=0,
    )
    grad_out_part = dot_tn(mixed, d_branch)
    grad_out_mine = core_half(grad_out_part) + partner(
        jnp.where(core == 0, grad_out_part[:, half:], grad_out_part[:, :half]).astype(bf16)
    ).astype(f32)
    grad_second = scatter_chips(
        jnp.concatenate([grad_out_mine.astype(bf16), grad_up_part], axis=1), pos
    )

    backs = [attend_back_pair(qkv, heads[p][1], d_mixed, p, pairs) for p in range(pairs)]
    d_project = jnp.concatenate([b[i] for i in range(3) for b in backs], axis=1)
    d_one_part = dot_nt(d_project, qkv_w)
    d_act_one = d_one_part[:own] + partner(d_one_part[own:])
    grad_qkv_part = dot_tn(act_one, d_project).astype(bf16)
    project_sum = column_sum(d_project)
    normed_own = normed_one[:own]
    grad_gain_one = jnp.sum(d_act_one * normed_own, axis=0)
    grad_shift_one = jnp.sum(d_act_one, axis=0)
    d_tokens = (d_middle + norm_back(d_act_one, normed_own, r_one[:own], gain_one)).astype(bf16)

    blank = jnp.zeros((half,), f32)
    sums = jnp.stack(
        [
            in_order(core, project_sum[:half], blank, 0),
            in_order(core, project_sum[2 * half :], blank, 0),
            grad_bias_out,
            column_sum(grad_out),
            grad_gain_one,
            grad_shift_one,
            grad_gain_two,
            grad_shift_two,
        ]
    )
    vec_grads = jnp.concatenate(
        [
            sums.T,
            grad_bias_up.reshape(chips * chip_rows, per_row),
            jnp.zeros((chips * chip_rows, LANES - 8 - per_row), f32),
        ],
        axis=1,
    ).astype(bf16)
    grad_first = scatter_chips(jnp.concatenate([grad_qkv_part, vec_grads], axis=1), pos)

    down_part = dot(hidden, down_w)
    result = (middle + (down_part[:own] + partner(down_part[own:])) + bd).astype(bf16)

    both = jnp.concatenate([grad_first, grad_second], axis=1)
    keep_rows = jnp.where(core == 0, both[:rows], both[rows:])
    came = partner(jnp.where(core == 0, both[rows:], both[:rows]))

    def columns(lo, hi):
        return keep_rows[:, lo:hi], came[:, lo:hi]

    qkv_pair = columns(0, 3 * half)
    grad_w_qkv = jnp.where(
        core == 0,
        jnp.stack([qkv_pair[0].reshape(rows, 3, half), qkv_pair[1].reshape(rows, 3, half)], 2),
        jnp.stack([qkv_pair[1].reshape(rows, 3, half), qkv_pair[0].reshape(rows, 3, half)], 2),
    ).reshape(rows, 3 * width)
    at = 3 * half
    vec_mine, vec_came = columns(at, at + 8)
    vec = (vec_mine + vec_came).T
    grad_bu = grad_first[:, at + 8 : at + 8 + per_row].reshape(strip)
    at += LANES
    grad_w_out = in_order(core, *columns(at, at + half), 1)
    at += half
    up_mine, up_came = (u.reshape(rows, chips, strip) for u in columns(at, at + ff_half))
    grad_w_up = jnp.where(
        core == 0, jnp.stack([up_mine, up_came], 2), jnp.stack([up_came, up_mine], 2)
    ).reshape(rows, 2 * ff_half)
    return (
        result,
        d_tokens,
        grad_w_qkv,
        vec[0],
        vec[1],
        grad_w_out,
        vec[2],
        grad_w_up,
        grad_bu,
        grad_down,
        vec[3],
        vec[4],
        vec[5],
        vec[6],
        vec[7],
    )


def solution(mesh):
    matrix, vector = P("dev", None), P("dev")
    in_specs = (
        matrix,
        vector,
        matrix,
        vector,
        vector,
        matrix,
        vector,
        matrix,
        vector,
        matrix,
        vector,
        vector,
        vector,
        vector,
        vector,
        matrix,
    )
    out_specs = (
        matrix,
        matrix,
        matrix,
        vector,
        vector,
        matrix,
        vector,
        matrix,
        vector,
        matrix,
        vector,
        vector,
        vector,
        vector,
        vector,
    )
    return jax.shard_map(
        on_device, mesh=mesh, in_specs=in_specs, out_specs=out_specs, check_vma=False
    )
```
